32 devices in a mesh: group: 2 (over x), seq: 16 (over z, y, core).
Axes of the slice: x: 2, y: 2, z: 4, core: 2. Of those that a mesh axis runs over, the one named last changes fastest.
Arguments:
- x_rows: bfloat16 [32, 8192], P('group', 'seq'), parts along dimension 0, may hold values from -0.59765625 to 0.59765625
- attn_gain: bfloat16 [8192], replicated, may hold values from 0.5 to 1.5
- q_weight: bfloat16 [8192, 8192], P(None, 'seq'), may hold values from -0.0625 to 0.0625
- o_weight: bfloat16 [8192, 8192], P('seq'), may hold values from -0.0625 to 0.0625
- mlp_gain: bfloat16 [8192], replicated, may hold values from 0.5 to 1.5
- gate_weight: bfloat16 [8192, 14336], P(None, 'seq'), may hold values from -0.0625 to 0.0625
- up_weight: bfloat16 [8192, 14336], P(None, 'seq'), may hold values from -0.0625 to 0.0625
- down_weight: bfloat16 [14336, 8192], P('seq'), may hold values from -0.046875 to 0.046875
- kv_cache: bfloat16 [2, 4096, 1024], P(None, ('group', 'seq')), parts along dimension 1, may hold values from -250 to 250, as said below
- block_mask: int32 [32, 8, 16], P('group', None, 'seq'), parts along dimension 0, may hold values from 0 to 1, as said below
Outputs:
- y_rows: bfloat16 [32, 8192], P('group', 'seq'), parts along dimension 0
The draws below stay inside these ranges and needn't reach their ends.
There are 2 independent parts, one for each index of `group`. The reference program is written for one: setup_inputs(seed, part) draws one part's arguments, and reference() takes and returns one part's arrays. A program takes and returns all parts, laid end to end along the dimension named above; an argument that names none is the same for every part. Nothing has to cross between parts.
Inputs may be any that keep to these rules, and one draw needn't show every extreme that they name: `kv_cache`: document keys and values; they differ from document to document. `block_mask`: 1 where the row may attend to that block of 128 document tokens for that key-value head, else 0; the document's last block is 1 for every row and key-value head.
All inputs are finite; a program needn't handle non-finite values.
Results may differ from the reference program's by a relative error of at most 0.013.
The reference program's roundings to bfloat16 on the way (of `normed`, `queries`, `attended`, `stream`, `normed_two` and `hidden`) count: a program that leaves them out, or rounds other values in their place, can miss the bound.
Values may be sent and summed in bfloat16 or wider, within the bound.
A program may use at most 192 MiB of HBM per device.

```python
import jax
import jax.numpy as jnp
from jax import lax

D = 8192
HEADS = 64
KV_HEADS = 8
HEAD_DIM = 128
FF_WIN = 14336
BLOCK = 128
ROWS = 16
KV_DEV = 128
DOC = 2048
NBLK = 16
N_SEQ = 16


def draw_kv_cache(key, part):
    width = KV_HEADS * HEAD_DIM
    keys = 1.5 * jnp.clip(jax.random.normal(jax.random.fold_in(key, 21), (DOC, width), jnp.float32), -4.0, 4.0)
    values = 4.0 * jnp.clip(jax.random.normal(jax.random.fold_in(key, 22), (DOC, width), jnp.float32), -4.0, 4.0)
    return jnp.stack([keys, values]).astype(jnp.bfloat16)


def draw_block_mask(key, part):
    position = jnp.arange(NBLK, dtype=jnp.int32)
    limit = 150 + 800 * position * position // (NBLK * NBLK)
    rolled = jax.random.randint(jax.random.fold_in(key, 31), (ROWS, KV_HEADS, NBLK), 0, 1000, jnp.int32)
    drawn = (rolled < limit[None, None, :]).astype(jnp.int32)
    last = (position == NBLK - 1)[None, None, :]
    return jnp.where(last, 1, drawn).astype(jnp.int32)


def levels(rng, extent, shards, low, high):
    loudness, own = 1.0, jax.random.fold_in(rng, 6)
    for axis_at, parts in shards:
        draws = jnp.exp(jax.random.uniform(jax.random.fold_in(own, axis_at), (parts,), jnp.float32, low / len(shards), high / len(shards)))
        loudness = loudness * jnp.repeat(draws, extent[axis_at] // parts).reshape([-1 if axis == axis_at else 1 for axis in range(len(extent))])
    return loudness


def gaussian(rng, dims, deviation, bound, split=(), kind=jnp.bfloat16):
    level = levels(rng, dims, split, -0.22, 0.18) if split else 1.0
    result = jax.random.normal(rng, dims, jnp.float32) * deviation * level
    return jnp.minimum(jnp.maximum(result, -bound), bound).astype(kind)


def setup_inputs(seed: int = 0, part: int = 0) -> dict:
    key_of = jax.random.split(jax.random.key(seed), 11)
    part_splits = jax.random.split(jax.random.fold_in(key_of[10], part), 11)
    return {
        "x_rows": gaussian(part_splits[0], (ROWS, D), 0.1, 0.59765625, ((1, 16),)),
        "attn_gain": jnp.clip(1.0 + 0.1 * jax.random.normal(key_of[1], (D,), jnp.float32), 0.5, 1.5).astype(jnp.bfloat16),
        "q_weight": gaussian(key_of[2], (D, HEADS * HEAD_DIM), D ** -0.5, 0.0625, ((1, 16),)),
        "o_weight": gaussian(key_of[3], (HEADS * HEAD_DIM, D), (HEADS * HEAD_DIM) ** -0.5, 0.0625, ((0, 16),)),
        "mlp_gain": jnp.clip(1.0 + 0.1 * jax.random.normal(key_of[4], (D,), jnp.float32), 0.5, 1.5).astype(jnp.bfloat16),
        "gate_weight": gaussian(key_of[5], (D, FF_WIN), D ** -0.5, 0.0625, ((1, 16),)),
        "up_weight": gaussian(key_of[6], (D, FF_WIN), D ** -0.5, 0.0625, ((1, 16),)),
        "down_weight": gaussian(key_of[7], (FF_WIN, D), FF_WIN ** -0.5, 0.046875, ((0, 16),)),
        "kv_cache": draw_kv_cache(jax.random.fold_in(jax.random.fold_in(key_of[10], part), 71), part),
        "block_mask": draw_block_mask(jax.random.fold_in(jax.random.fold_in(key_of[10], part), 71), part),
    }


eps = 1e-05
floor_score = -1e+30

def rms_norm(values, gain):
    wide = values.astype(jnp.float32)
    inverse = lax.rsqrt(lax.optimization_barrier(jnp.mean(wide * wide, axis=-1, keepdims=True)) + eps)
    return (wide * inverse * gain.astype(jnp.float32)).astype(jnp.bfloat16)

def reference(x_rows, attn_gain, q_weight, o_weight, mlp_gain, gate_weight, up_weight, down_weight, kv_cache, block_mask):
    rows = x_rows.shape[0]
    group = HEADS // KV_HEADS
    spans = KV_DEV // BLOCK
    scale = 1.0 / HEAD_DIM ** 0.5
    normed = rms_norm(x_rows, attn_gain)
    queries = jnp.dot(normed, q_weight, preferred_element_type=jnp.float32).astype(jnp.bfloat16)
    query_wide = queries.reshape(rows, KV_HEADS, group, HEAD_DIM).astype(jnp.float32)
    doc_keys = kv_cache[0]
    doc_values = kv_cache[1]

    def one_span(carry, index):
        top, total, accum = carry
        start = (index * KV_DEV).astype(jnp.int32)
        span_keys = lax.dynamic_slice_in_dim(doc_keys, start, KV_DEV, 0).reshape(KV_DEV, KV_HEADS, HEAD_DIM).astype(jnp.float32)
        span_values = lax.dynamic_slice_in_dim(doc_values, start, KV_DEV, 0).reshape(KV_DEV, KV_HEADS, HEAD_DIM).astype(jnp.float32)
        span_mask = lax.dynamic_slice_in_dim(block_mask, (index * spans).astype(jnp.int32), spans, 2)
        scores = jnp.einsum('rghd,kgd->rghk', query_wide, span_keys) * scale
        scores = scores.reshape(rows, KV_HEADS, group, spans, BLOCK)
        live = (span_mask == 1)[:, :, None, :, None]
        masked = jnp.where(live, scores, floor_score)
        local_top = lax.optimization_barrier(jnp.max(masked, axis=(3, 4)))
        weights = jnp.where(live, jnp.exp(masked - local_top[..., None, None]), 0.0)
        local_total = lax.optimization_barrier(jnp.sum(weights, axis=(3, 4)))
        rounded = lax.optimization_barrier(weights.astype(jnp.bfloat16)).astype(jnp.float32)
        rounded = rounded.reshape(rows, KV_HEADS, group, KV_DEV)
        local_accum = jnp.einsum('rghk,kgd->rghd', rounded, span_values)
        new_top = jnp.maximum(top, local_top)
        old_factor = jnp.exp(top - new_top)
        new_factor = jnp.exp(local_top - new_top)
        total = total * old_factor + local_total * new_factor
        accum = accum * old_factor[..., None] + local_accum * new_factor[..., None]
        return ((new_top, total, accum), None)
    init = (jnp.full((rows, KV_HEADS, group), floor_score, jnp.float32), jnp.zeros((rows, KV_HEADS, group), jnp.float32), jnp.zeros((rows, KV_HEADS, group, HEAD_DIM), jnp.float32))
    (top, total, accum), _ = lax.scan(one_span, init, jnp.arange(N_SEQ, dtype=jnp.int32))
    attended = accum / total[..., None]
    attended = attended.reshape(rows, HEADS * HEAD_DIM).astype(jnp.bfloat16)
    stream = (x_rows.astype(jnp.float32) + jnp.dot(attended, o_weight, preferred_element_type=jnp.float32)).astype(jnp.bfloat16)
    normed_two = rms_norm(stream, mlp_gain)
    gate = jnp.dot(normed_two, gate_weight, preferred_element_type=jnp.float32)
    upward = jnp.dot(normed_two, up_weight, preferred_element_type=jnp.float32)
    hidden = (jax.nn.silu(gate) * upward).astype(jnp.bfloat16)
    return (stream.astype(jnp.float32) + jnp.dot(hidden, down_weight, preferred_element_type=jnp.float32)).astype(jnp.bfloat16)
```

```python
import functools

import jax
import jax.numpy as jnp
from jax import lax
from jax.experimental import pallas as pl
from jax.experimental.pallas import tpu as pltpu
from jax.sharding import PartitionSpec as P

HEADS = 64
KV_HEADS = 8
HEAD_DIM = 128
BLOCK = 128


eps = 1e-05
floor_score = -1e30


def combined_all(x, axis, combine):
    everything = jax.tree.map(lambda part: lax.all_gather(part, axis), x)
    initial = jax.tree.map(lambda part: part[0], everything)

    def turn(k, so_far):
        return combine(so_far, jax.tree.map(lambda part: part[k], everything))

    return lax.fori_loop(1, lax.axis_size(axis), turn, initial)


def rms_norm(values, gain):
    wide = values.astype(jnp.float32)
    inverse = lax.rsqrt(jnp.mean(wide * wide, axis=-1, keepdims=True) + eps)
    return (wide * inverse * gain.astype(jnp.float32)).astype(jnp.bfloat16)


def combine_states(first, second):
    top_a, total_a, accum_a = first
    top_b, total_b, accum_b = second
    top = jnp.maximum(top_a, top_b)
    factor_a = jnp.exp(top_a - top)
    factor_b = jnp.exp(top_b - top)
    return (
        top,
        total_a * factor_a + total_b * factor_b,
        accum_a * factor_a[..., None] + accum_b * factor_b[..., None],
    )


def local(
    x_rows,
    attn_gain,
    q_weight,
    o_weight,
    mlp_gain,
    gate_weight,
    up_weight,
    down_weight,
    kv_cache,
    block_mask,
):
    rows = x_rows.shape[0]
    group = HEADS // KV_HEADS
    key_len = kv_cache.shape[1]
    spans = key_len // BLOCK
    scale = 1.0 / HEAD_DIM**0.5
    whole = lax.all_gather(x_rows, "seq", axis=1, tiled=True)
    normed = rms_norm(whole, attn_gain)
    query_part = jnp.dot(normed, q_weight, preferred_element_type=jnp.float32).astype(jnp.bfloat16)
    queries = lax.all_gather(query_part, "seq", axis=1, tiled=True)
    doc_keys = kv_cache[0]
    doc_values = kv_cache[1]

    def one_group(index):
        query_group = lax.dynamic_slice_in_dim(
            queries, index * (group * HEAD_DIM), group * HEAD_DIM, 1
        ).reshape(rows, group, HEAD_DIM)
        key_group = lax.dynamic_slice_in_dim(doc_keys, index * HEAD_DIM, HEAD_DIM, 1)
        value_group = lax.dynamic_slice_in_dim(doc_values, index * HEAD_DIM, HEAD_DIM, 1)
        mask_group = lax.dynamic_slice_in_dim(block_mask, index, 1, 1)[:, 0, :]
        scores = (
            jnp.einsum("rhd,kd->rhk", query_group, key_group, preferred_element_type=jnp.float32)
            * scale
        )
        scores = scores.reshape(rows, group, spans, BLOCK)
        live = (mask_group == 1)[:, None, :, None]
        masked = jnp.where(live, scores, floor_score)
        local_top = jnp.max(masked, axis=(2, 3))
        weights = jnp.where(live, jnp.exp(masked - local_top[..., None, None]), 0.0)
        local_total = jnp.sum(weights, axis=(2, 3))
        rounded = weights.astype(jnp.bfloat16).reshape(rows, group, key_len)
        local_accum = jnp.einsum(
            "rhk,kd->rhd", rounded, value_group, preferred_element_type=jnp.float32
        )
        return (local_top, local_total, local_accum)

    tops, totals, accums = lax.map(one_group, jnp.arange(KV_HEADS, dtype=jnp.int32))
    local_top = jnp.moveaxis(tops, 0, 1)
    local_total = jnp.moveaxis(totals, 0, 1)
    local_accum = jnp.moveaxis(accums, 0, 1)
    columns = q_weight.shape[1]
    col_start = lax.axis_index("seq") * columns
    top, total, accum = combined_all((local_top, local_total, local_accum), "seq", combine_states)
    attended = accum / total[..., None]
    attended = attended.reshape(rows, HEADS * HEAD_DIM).astype(jnp.bfloat16)
    attn_cols = lax.dynamic_slice_in_dim(attended, col_start, columns, 1)
    weight_cols = o_weight
    attn_out = lax.psum_scatter(
        lax.dot_general(
            weight_cols, attn_cols, (((0,), (1,)), ((), ())), preferred_element_type=jnp.float32
        ),
        "seq",
        scatter_dimension=0,
        tiled=True,
    )
    stream = (x_rows.astype(jnp.float32) + attn_out.T).astype(jnp.bfloat16)
    stream_whole = lax.all_gather(stream, "seq", axis=1, tiled=True)
    normed_two = rms_norm(stream_whole, mlp_gain)
    gate = jnp.dot(normed_two, gate_weight, preferred_element_type=jnp.float32)
    upward = jnp.dot(normed_two, up_weight, preferred_element_type=jnp.float32)
    hidden = (jax.nn.silu(gate) * upward).astype(jnp.bfloat16)
    weight_cols = down_weight
    down_out = lax.psum_scatter(
        lax.dot_general(
            weight_cols, hidden, (((0,), (1,)), ((), ())), preferred_element_type=jnp.float32
        ),
        "seq",
        scatter_dimension=0,
        tiled=True,
    )
    return (stream.astype(jnp.float32) + down_out.T).astype(jnp.bfloat16)


SCALE = 1.0 / HEAD_DIM**0.5
MASK_AT = 2 * BLOCK


def layer_kernel(
    x_hbm,
    gain_one_hbm,
    q_hbm,
    o_hbm,
    gain_two_hbm,
    gate_hbm,
    up_hbm,
    down_hbm,
    kv_hbm,
    mask_hbm,
    y_ref,
    q_w,
    o_w,
    gate_w,
    up_w,
    down_w,
    gain_one,
    gain_two,
    mask_ref,
    x_all,
    s_all,
    normed,
    kv_stage,
    kv_all,
    scores,
    q_own,
    q_got,
    piece,
    piece_got,
    duo_one,
    duo_got_one,
    part_one,
    got_one,
    duo_two,
    duo_got_two,
    part_two,
    got_two,
    own_ref,
    w_sem,
    in_sem,
    stage_sem,
    kv_own_sem,
    x_send,
    x_recv,
    x_pass,
    s_send,
    s_recv,
    s_pass,
    kv_send,
    kv_recv,
    q_send,
    q_recv,
    piece_send,
    piece_recv,
    duo_send_one,
    duo_recv_one,
    send_one,
    recv_one,
    duo_send_two,
    duo_recv_two,
    send_two,
    recv_two,
):
    devices, rows, cols = x_all.shape
    chips = devices // 2
    near = chips // 2
    group = cols // HEAD_DIM
    lines = group * rows
    me = lax.axis_index("seq")
    chip = me // 2
    core = me % 2
    partner = chip * 2 + 1 - core
    half = chip // near
    spot = chip % near
    mirror = (chip + near) % chips
    lane = me % chips

    def remote(src, dst, send, recv, device):
        return pltpu.make_async_remote_copy(
            src_ref=src,
            dst_ref=dst,
            send_sem=send,
            recv_sem=recv,
            device_id={"seq": device},
            device_id_type=pl.DeviceIdType.MESH,
        )

    def step_off(s):
        return chips // 2 + ((s + 1) // 2) * (1 - 2 * (s % 2))

    far_first = [step_off(s) for s in range(chips - 1)]

    def chip_at(off):
        return (chip + off) % chips

    barrier = pltpu.get_barrier_semaphore()
    for off in range(1, devices):
        pl.semaphore_signal(
            barrier,
            inc=1,
            device_id={"seq": (me + off) % devices},
            device_id_type=pl.DeviceIdType.MESH,
        )

    load_x = pltpu.make_async_copy(x_hbm, x_all.at[me], in_sem.at[0])
    load_mask = pltpu.make_async_copy(mask_hbm, mask_ref, in_sem.at[1])
    load_gain_one = pltpu.make_async_copy(gain_one_hbm, gain_one, in_sem.at[2])
    load_gain_two = pltpu.make_async_copy(gain_two_hbm, gain_two, in_sem.at[3])
    load_x.start()
    load_mask.start()
    stages = []
    for g in range(KV_HEADS):
        for side in range(2):
            stages.append(
                pltpu.make_async_copy(
                    kv_hbm.at[side, :, pl.ds(g * HEAD_DIM, HEAD_DIM)],
                    kv_stage.at[g // near, g % near, pl.ds(side * BLOCK, BLOCK)],
                    stage_sem.at[2 * g + side],
                )
            )
            stages[-1].start()
    load_gain_one.start()
    load_gain_two.start()

    def fetch(k, src, dst):
        return pltpu.make_async_copy(src, dst, w_sem.at[k])

    fetch_q = fetch(0, q_hbm, q_w)
    fetch_o = fetch(1, o_hbm, o_w)
    fetch_gate = fetch(2, gate_hbm, gate_w)
    fetch_up = fetch(3, up_hbm, up_w)
    fetch_down = fetch(4, down_hbm, down_w)
    fetch_q.start()
    fetch_o.start()

    load_mask.wait()
    across = lax.broadcasted_iota(jnp.int32, (rows, rows), 1)
    down = lax.broadcasted_iota(jnp.int32, (rows, rows), 0)
    for g in range(KV_HEADS):
        flat = jnp.broadcast_to(mask_ref[g].astype(jnp.float32), (rows, rows))
        column = jnp.sum(jnp.where(across == down, flat, 0.0), axis=1, keepdims=True)
        kv_stage[g // near, g % near, pl.ds(MASK_AT, rows), :] = jnp.broadcast_to(
            column, (rows, HEAD_DIM)
        ).astype(jnp.bfloat16)
    load_x.wait()
    for stage in stages:
        stage.wait()
    own_kv = pltpu.make_async_copy(kv_stage.at[core, spot], kv_all.at[lane], kv_own_sem)
    own_kv.start()
    with jax.named_scope("t_barrier"):
        pl.semaphore_wait(barrier, devices - 1)

    def gather_start(dst, send, recv):
        for off in far_first:
            remote(
                dst.at[me], dst.at[me], send.at[off], recv.at[me], chip_at(off) * 2 + core
            ).start()
        remote(dst.at[me], dst.at[me], send.at[0], recv.at[me], partner).start()

    def gather_pass(dst, send, recv, hand):
        for off in reversed(far_first):
            other = chip_at(off) * 2 + core
            remote(dst.at[other], dst.at[other], send.at[off], recv.at[other], partner).wait_recv()
            remote(dst.at[other], dst.at[other], hand.at[off], recv.at[other], partner).start()

    def gather_finish(dst, send, recv):
        for off in range(chips):
            other = chip_at(off) * 2 + 1 - core
            remote(dst.at[other], dst.at[other], send.at[0], recv.at[other], partner).wait_recv()

    def gather_drain(dst, send, recv, hand):
        for off in range(chips):
            remote(dst.at[me], dst.at[me], send.at[off], recv.at[me], partner).wait_send()
        for off in far_first:
            remote(dst.at[me], dst.at[me], hand.at[off], recv.at[me], partner).wait_send()

    gather_start(x_all, x_send, x_recv)

    for k in range(chips - 1, 0, -1):
        there = (spot + k // 2) % near
        side = (core + k) % 2
        remote(
            kv_stage.at[side, there],
            kv_all.at[lane],
            kv_send.at[k],
            kv_recv.at[lane],
            (half * near + there) * 2 + side,
        ).start()
    fetch_gate.start()
    fetch_up.start()
    fetch_down.start()

    def norm(values, gain):
        squares = jnp.zeros((rows, cols), jnp.float32)
        for i in range(devices):
            wide = values[i].astype(jnp.float32)
            squares = squares + wide * wide
        mean = jnp.sum(squares, axis=-1, keepdims=True) * (1.0 / (devices * cols))
        inverse = lax.rsqrt(mean + eps)
        for i in range(devices):
            part_gain = gain[i * cols : (i + 1) * cols].astype(jnp.float32).reshape(1, cols)
            normed[i] = (values[i].astype(jnp.float32) * inverse * part_gain).astype(jnp.bfloat16)

    with jax.named_scope("t_xgather"):
        gather_pass(x_all, x_send, x_recv, x_pass)
        load_gain_one.wait()
        load_gain_two.wait()
        gather_finish(x_all, x_send, x_recv)
    norm(x_all, gain_one)
    with jax.named_scope("t_fetchq"):
        fetch_q.wait()
    step = 4

    def q_step(t, total):
        for u in range(step):
            i = t * step + u
            total = total + jnp.dot(
                normed[i],
                q_w[pl.ds(pl.multiple_of(i * cols, cols), cols), :],
                preferred_element_type=jnp.float32,
            )
        return total

    with jax.named_scope("t_qmm"):
        queries = lax.fori_loop(
            0, devices // step, q_step, jnp.zeros((rows, cols), jnp.float32)
        ).astype(jnp.bfloat16)
        q_own[...] = jnp.concatenate(
            [queries[:, h * HEAD_DIM : (h + 1) * HEAD_DIM] for h in range(group)], axis=0
        )

    keeps = core == half
    to_mirror = remote(
        q_own, q_got.at[core], q_send.at[0], q_recv.at[core], mirror * 2 + half
    )
    to_partner = remote(q_own, q_got.at[core], q_send.at[1], q_recv.at[core], partner)
    to_mirror.start()

    @pl.when(jnp.logical_not(keeps))
    def _():
        to_partner.start()

    @pl.when(keeps)
    def _():
        q_got[core] = q_own[...]

    with jax.named_scope("t_kvwait"):
        own_kv.wait()
        for c in range(1, chips):
            other = (lane + c) % chips
            remote(
                kv_all.at[other], kv_all.at[other], kv_send.at[0], kv_recv.at[other], partner
            ).wait_recv()

    def q_arrived(which):
        remote(q_own, q_got.at[which], q_send.at[0], q_recv.at[which], partner).wait_recv()

    with jax.named_scope("t_qwait"):
        q_arrived(1 - core)

        @pl.when(jnp.logical_not(keeps))
        def _():
            q_arrived(core)

    tops = []
    with jax.named_scope("t_attn"):
        query = jnp.concatenate([q_got[0], q_got[1]], axis=0)

        def live_at(c):
            mask = kv_all[c, pl.ds(MASK_AT, rows), :].astype(jnp.float32)
            return jnp.concatenate([mask] * (2 * group), axis=0) > 0.5

        for c in range(chips):
            score = (
                lax.dot_general(
                    query,
                    kv_all[c, pl.ds(0, BLOCK), :],
                    (((1,), (1,)), ((), ())),
                    preferred_element_type=jnp.float32,
                )
                * SCALE
            )
            masked = jnp.where(live_at(c), score, floor_score)
            scores[c] = masked
            tops.append(jnp.max(masked, axis=-1, keepdims=True))
        top = functools.reduce(jnp.maximum, tops)
        total = jnp.zeros((2 * lines, 1), jnp.float32)
        accum = jnp.zeros((2 * lines, HEAD_DIM), jnp.float32)
        for c in range(chips):
            weight = jnp.where(live_at(c), jnp.exp(scores[c] - tops[c]), 0.0)
            factor = jnp.exp(tops[c] - top)
            total = total + factor * jnp.sum(weight, axis=-1, keepdims=True)
            accum = accum + factor * jnp.dot(
                weight.astype(jnp.bfloat16),
                kv_all[c, pl.ds(BLOCK, BLOCK), :],
                preferred_element_type=jnp.float32,
            )
        row = lax.broadcasted_iota(jnp.int32, (lines, HEAD_DIM), 0)
        column = lax.broadcasted_iota(jnp.int32, (lines, HEAD_DIM), 1)
        for s in range(2):
            at = slice(s * lines, (s + 1) * lines)
            spread = jnp.where(
                column == row, top[at], jnp.where(column == row + lines, total[at], 0.0)
            )
            piece[s, pl.ds(0, lines), :] = accum[at]
            piece[s, pl.ds(lines, 8), :] = jnp.broadcast_to(
                jnp.sum(spread, axis=0, keepdims=True), (8, HEAD_DIM)
            )

    def piece_copy(which, slot, device):
        return remote(
            piece.at[which], piece_got.at[slot], piece_send.at[which], piece_recv.at[slot], device
        )

    @pl.when(keeps)
    def _():
        piece_copy(1 - core, 0, partner).start()
        piece_got[0] = piece[core]

    @pl.when(jnp.logical_not(keeps))
    def _():
        piece_copy(0, 1, mirror * 2).start()
        piece_copy(1, 1, mirror * 2 + 1).start()

    with jax.named_scope("t_piece"):

        @pl.when(jnp.logical_not(keeps))
        def _():
            piece_copy(0, 0, partner).wait_recv()

        piece_copy(0, 1, partner).wait_recv()

    with jax.named_scope("t_join"):

        def parts_of(slot):
            stats = jnp.broadcast_to(piece_got[slot, pl.ds(lines, 1), :], (lines, HEAD_DIM))
            high = jnp.sum(jnp.where(column == row, stats, 0.0), axis=1, keepdims=True)
            mass = jnp.sum(jnp.where(column == row + lines, stats, 0.0), axis=1, keepdims=True)
            return high, mass, piece_got[slot, pl.ds(0, lines), :]

        top_a, total_a, accum_a = parts_of(0)
        top_b, total_b, accum_b = parts_of(1)
        high = jnp.maximum(top_a, top_b)
        factor_a = jnp.exp(top_a - high)
        factor_b = jnp.exp(top_b - high)
        ratio = (accum_a * factor_a + accum_b * factor_b) / (
            total_a * factor_a + total_b * factor_b
        )
        attended = jnp.concatenate(
            [ratio[h * rows : (h + 1) * rows] for h in range(group)], axis=1
        ).astype(jnp.bfloat16)

    def scatter(values, weight, duo, duo_got, duo_send, duo_recv, part, got, send, recv):
        def product(to):
            return jnp.dot(
                values,
                weight[:, pl.ds(pl.multiple_of(to * cols, cols), cols)],
                preferred_element_type=jnp.float32,
            )

        def give(s):
            return remote(duo.at[s], duo_got.at[s], duo_send.at[s], duo_recv.at[s], partner)

        def post(s):
            return remote(
                part.at[s],
                got.at[chip],
                send.at[s],
                recv.at[chip],
                chip_at(step_off(s)) * 2 + core,
            )

        def turn_one(t, _):
            first = product(chip_at(step_off(2 * t)) * 2 + 1 - core)
            second = product(chip_at(step_off(2 * t + 1)) * 2 + 1 - core)
            duo[2 * t] = first
            duo[2 * t + 1] = second

            @pl.when(t > 0)
            def _():
                give(2 * t - 2).start()
                give(2 * t - 1).start()

            return 0

        def turn_two(t, _):
            first = product(chip_at(step_off(2 * t)) * 2 + core)
            second = product(chip_at(step_off(2 * t + 1)) * 2 + core)
            give(2 * t).wait_recv()
            give(2 * t + 1).wait_recv()
            first = first + duo_got[2 * t]
            second = second + duo_got[2 * t + 1]
            part[2 * t] = first.astype(part.dtype)
            part[2 * t + 1] = second.astype(part.dtype)
            own_ref[...] = second

            @pl.when(t > 0)
            def _():
                post(2 * t - 2).start()
                post(2 * t - 1).start()

            return 0

        with jax.named_scope("t_prod1"):
            lax.fori_loop(0, chips // 2, turn_one, 0)
            give(chips - 2).start()
            give(chips - 1).start()
        with jax.named_scope("t_prod2"):
            lax.fori_loop(0, chips // 2, turn_two, 0)
            post(chips - 2).start()

        total = own_ref[...]
        for s in range(chips - 2, -1, -1):
            other = chip_at(step_off(s))
            remote(
                part.at[s], got.at[other], send.at[s], recv.at[other], other * 2 + core
            ).wait_recv()
            total = total + got[other].astype(jnp.float32)
        return total

    def scatter_drain(duo, duo_got, duo_send, duo_recv, part, got, send, recv):
        for s in range(chips):
            remote(duo.at[s], duo_got.at[s], duo_send.at[s], duo_recv.at[s], partner).wait_send()
        for s in range(chips - 1):
            remote(part.at[s], got.at[chip], send.at[s], recv.at[chip], partner).wait_send()

    one = (duo_one, duo_got_one, duo_send_one, duo_recv_one, part_one, got_one, send_one, recv_one)
    two = (duo_two, duo_got_two, duo_send_two, duo_recv_two, part_two, got_two, send_two, recv_two)
    with jax.named_scope("t_fetcho"):
        fetch_o.wait()
    with jax.named_scope("t_scat1"):
        attn_out = scatter(attended, o_w, *one)
    stream = (x_all[me].astype(jnp.float32) + attn_out).astype(jnp.bfloat16)
    s_all[me] = stream
    gather_start(s_all, s_send, s_recv)
    with jax.named_scope("t_sgather"):
        gather_pass(s_all, s_send, s_recv, s_pass)
        gather_finish(s_all, s_send, s_recv)
    norm(s_all, gain_two)
    with jax.named_scope("t_fetchgu"):
        fetch_gate.wait()
        fetch_up.wait()
    wide = gate_w.shape[1]

    def ff_step(t, sums):
        gate, upward = sums
        for u in range(2):
            i = t * 2 + u
            at = pl.ds(pl.multiple_of(i * cols, cols), cols)
            gate = gate + jnp.dot(normed[i], gate_w[at, :], preferred_element_type=jnp.float32)
            upward = upward + jnp.dot(normed[i], up_w[at, :], preferred_element_type=jnp.float32)
        return gate, upward

    zeros = jnp.zeros((rows, wide), jnp.float32)
    with jax.named_scope("t_ffmm"):
        gate, upward = lax.fori_loop(0, devices // 2, ff_step, (zeros, zeros))
    hidden = (gate / (1.0 + jnp.exp(-gate)) * upward).astype(jnp.bfloat16)
    with jax.named_scope("t_fetchd"):
        fetch_down.wait()
    with jax.named_scope("t_scat2"):
        down_out = scatter(hidden, down_w, *two)
    y_ref[...] = (s_all[me].astype(jnp.float32) + down_out).astype(jnp.bfloat16)

    with jax.named_scope("t_drain"):
        gather_drain(x_all, x_send, x_recv, x_pass)
        gather_drain(s_all, s_send, s_recv, s_pass)
        for k in range(1, chips):
            remote(
                kv_stage.at[0, 0], kv_all.at[lane], kv_send.at[k], kv_recv.at[lane], partner
            ).wait_send()
        to_mirror.wait_send()

        @pl.when(jnp.logical_not(keeps))
        def _():
            to_partner.wait_send()
            piece_copy(0, 1, partner).wait_send()
            piece_copy(1, 1, partner).wait_send()

        @pl.when(keeps)
        def _():
            piece_copy(1 - core, 0, partner).wait_send()

        scatter_drain(*one)
        scatter_drain(*two)


def layer(
    x_rows,
    attn_gain,
    q_weight,
    o_weight,
    mlp_gain,
    gate_weight,
    up_weight,
    down_weight,
    kv_cache,
    block_mask,
):
    rows, cols = x_rows.shape
    devices = lax.axis_size("seq")
    chips = devices // 2
    lines = rows * cols // HEAD_DIM
    dma = pltpu.SemaphoreType.DMA
    left = pl.BlockSpec(memory_space=pl.ANY)
    exchange = pltpu.VMEM((devices, rows, cols), jnp.bfloat16)
    duo = pltpu.VMEM((chips, rows, cols), jnp.float32)
    part = pltpu.VMEM((chips, rows, cols), jnp.bfloat16)
    pieces = pltpu.VMEM((2, lines + 8, HEAD_DIM), jnp.float32)
    return pl.pallas_call(
        layer_kernel,
        name="layer",
        out_shape=jax.ShapeDtypeStruct((rows, cols), jnp.bfloat16),
        in_specs=[left] * 10,
        out_specs=pl.BlockSpec(memory_space=pltpu.VMEM),
        scratch_shapes=[
            pltpu.VMEM(q_weight.shape, jnp.bfloat16),
            pltpu.VMEM(o_weight.shape, jnp.bfloat16),
            pltpu.VMEM(gate_weight.shape, jnp.bfloat16),
            pltpu.VMEM(up_weight.shape, jnp.bfloat16),
            pltpu.VMEM(down_weight.shape, jnp.bfloat16),
            pltpu.VMEM(attn_gain.shape, jnp.bfloat16),
            pltpu.VMEM(mlp_gain.shape, jnp.bfloat16),
            pltpu.VMEM((KV_HEADS, 1, rows), jnp.int32),
            exchange,
            exchange,
            exchange,
            pltpu.VMEM((2, chips // 2, MASK_AT + rows, HEAD_DIM), jnp.bfloat16),
            pltpu.VMEM((chips, MASK_AT + rows, HEAD_DIM), jnp.bfloat16),
            pltpu.VMEM((chips, 2 * lines, BLOCK), jnp.float32),
            pltpu.VMEM((lines, HEAD_DIM), jnp.bfloat16),
            pltpu.VMEM((2, lines, HEAD_DIM), jnp.bfloat16),
            pieces,
            pieces,
            *([duo, duo, part, part] * 2),
            pltpu.VMEM((rows, cols), jnp.float32),
            dma((5,)),
            dma((4,)),
            dma((2 * KV_HEADS,)),
            dma(()),
            *([dma((chips,)), dma((devices,)), dma((chips,))] * 2),
            dma((chips,)),
            dma((chips,)),
            *([dma((2,))] * 4),
            *([dma((chips,))] * 8),
        ],
        compiler_params=pltpu.CompilerParams(
            collective_id=0, has_side_effects=True, vmem_limit_bytes=67043328
        ),
    )(
        x_rows,
        attn_gain,
        q_weight,
        o_weight,
        mlp_gain,
        gate_weight,
        up_weight,
        down_weight,
        kv_cache,
        jnp.transpose(block_mask, (1, 2, 0)),
    )


def solution(mesh):
    fused = mesh.shape["seq"] == 2 * KV_HEADS
    return jax.shard_map(
        layer if fused else local,
        mesh=mesh,
        in_specs=(
            P("group", "seq"),
            P(),
            P(None, "seq"),
            P("seq", None),
            P(),
            P(None, "seq"),
            P(None, "seq"),
            P("seq", None),
            P(None, ("group", "seq"), None),
            P("group", None, "seq"),
        ),
        out_specs=P("group", "seq"),
        check_vma=False,
    )
```

```python
import functools

import jax
import jax.numpy as jnp
from jax import lax
from jax.experimental import pallas as pl
from jax.experimental.pallas import tpu as pltpu
from jax.sharding import PartitionSpec as P

HEADS = 64
KV_HEADS = 8
HEAD_DIM = 128
BLOCK = 128


eps = 1e-05
floor_score = -1e30


def combined_all(x, axis, combine):
    everything = jax.tree.map(lambda part: lax.all_gather(part, axis), x)
    initial = jax.tree.map(lambda part: part[0], everything)

    def turn(k, so_far):
        return combine(so_far, jax.tree.map(lambda part: part[k], everything))

    return lax.fori_loop(1, lax.axis_size(axis), turn, initial)


def rms_norm(values, gain):
    wide = values.astype(jnp.float32)
    inverse = lax.rsqrt(jnp.mean(wide * wide, axis=-1, keepdims=True) + eps)
    return (wide * inverse * gain.astype(jnp.float32)).astype(jnp.bfloat16)


def combine_states(first, second):
    top_a, total_a, accum_a = first
    top_b, total_b, accum_b = second
    top = jnp.maximum(top_a, top_b)
    factor_a = jnp.exp(top_a - top)
    factor_b = jnp.exp(top_b - top)
    return (
        top,
        total_a * factor_a + total_b * factor_b,
        accum_a * factor_a[..., None] + accum_b * factor_b[..., None],
    )


def local(
    x_rows,
    attn_gain,
    q_weight,
    o_weight,
    mlp_gain,
    gate_weight,
    up_weight,
    down_weight,
    kv_cache,
    block_mask,
):
    rows = x_rows.shape[0]
    group = HEADS // KV_HEADS
    key_len = kv_cache.shape[1]
    spans = key_len // BLOCK
    scale = 1.0 / HEAD_DIM**0.5
    whole = lax.all_gather(x_rows, "seq", axis=1, tiled=True)
    normed = rms_norm(whole, attn_gain)
    query_part = jnp.dot(normed, q_weight, preferred_element_type=jnp.float32).astype(jnp.bfloat16)
    queries = lax.all_gather(query_part, "seq", axis=1, tiled=True)
    doc_keys = kv_cache[0]
    doc_values = kv_cache[1]

    def one_group(index):
        query_group = lax.dynamic_slice_in_dim(
            queries, index * (group * HEAD_DIM), group * HEAD_DIM, 1
        ).reshape(rows, group, HEAD_DIM)
        key_group = lax.dynamic_slice_in_dim(doc_keys, index * HEAD_DIM, HEAD_DIM, 1)
        value_group = lax.dynamic_slice_in_dim(doc_values, index * HEAD_DIM, HEAD_DIM, 1)
        mask_group = lax.dynamic_slice_in_dim(block_mask, index, 1, 1)[:, 0, :]
        scores = (
            jnp.einsum("rhd,kd->rhk", query_group, key_group, preferred_element_type=jnp.float32)
            * scale
        )
        scores = scores.reshape(rows, group, spans, BLOCK)
        live = (mask_group == 1)[:, None, :, None]
        masked = jnp.where(live, scores, floor_score)
        local_top = jnp.max(masked, axis=(2, 3))
        weights = jnp.where(live, jnp.exp(masked - local_top[..., None, None]), 0.0)
        local_total = jnp.sum(weights, axis=(2, 3))
        rounded = weights.astype(jnp.bfloat16).reshape(rows, group, key_len)
        local_accum = jnp.einsum(
            "rhk,kd->rhd", rounded, value_group, preferred_element_type=jnp.float32
        )
        return (local_top, local_total, local_accum)

    tops, totals, accums = lax.map(one_group, jnp.arange(KV_HEADS, dtype=jnp.int32))
    local_top = jnp.moveaxis(tops, 0, 1)
    local_total = jnp.moveaxis(totals, 0, 1)
    local_accum = jnp.moveaxis(accums, 0, 1)
    columns = q_weight.shape[1]
    col_start = lax.axis_index("seq") * columns
    top, total, accum = combined_all((local_top, local_total, local_accum), "seq", combine_states)
    attended = accum / total[..., None]
    attended = attended.reshape(rows, HEADS * HEAD_DIM).astype(jnp.bfloat16)
    attn_cols = lax.dynamic_slice_in_dim(attended, col_start, columns, 1)
    weight_cols = o_weight
    attn_out = lax.psum_scatter(
        lax.dot_general(
            weight_cols, attn_cols, (((0,), (1,)), ((), ())), preferred_element_type=jnp.float32
        ),
        "seq",
        scatter_dimension=0,
        tiled=True,
    )
    stream = (x_rows.astype(jnp.float32) + attn_out.T).astype(jnp.bfloat16)
    stream_whole = lax.all_gather(stream, "seq", axis=1, tiled=True)
    normed_two = rms_norm(stream_whole, mlp_gain)
    gate = jnp.dot(normed_two, gate_weight, preferred_element_type=jnp.float32)
    upward = jnp.dot(normed_two, up_weight, preferred_element_type=jnp.float32)
    hidden = (jax.nn.silu(gate) * upward).astype(jnp.bfloat16)
    weight_cols = down_weight
    down_out = lax.psum_scatter(
        lax.dot_general(
            weight_cols, hidden, (((0,), (1,)), ((), ())), preferred_element_type=jnp.float32
        ),
        "seq",
        scatter_dimension=0,
        tiled=True,
    )
    return (stream.astype(jnp.float32) + down_out.T).astype(jnp.bfloat16)


SCALE = 1.0 / HEAD_DIM**0.5
MASK_AT = 2 * BLOCK


def layer_kernel(
    x_hbm,
    gain_one_hbm,
    q_hbm,
    o_hbm,
    gain_two_hbm,
    gate_hbm,
    up_hbm,
    down_hbm,
    kv_hbm,
    mask_hbm,
    y_ref,
    q_w,
    o_w,
    gate_w,
    up_w,
    down_w,
    gain_one,
    gain_two,
    mask_ref,
    x_all,
    s_all,
    normed,
    kv_stage,
    kv_all,
    scores,
    q_own,
    q_got,
    piece,
    piece_got,
    duo_one,
    duo_got_one,
    part_one,
    got_one,
    duo_two,
    duo_got_two,
    part_two,
    got_two,
    own_ref,
    w_sem,
    in_sem,
    stage_sem,
    kv_own_sem,
    x_send,
    x_near,
    x_far,
    s_send,
    s_near,
    s_far,
    kv_send,
    kv_recv,
    q_send,
    q_recv,
    piece_send,
    piece_recv,
    duo_send_one,
    duo_recv_one,
    send_one,
    recv_one,
    duo_send_two,
    duo_recv_two,
    send_two,
    recv_two,
):
    devices, rows, cols = x_all.shape
    chips = devices // 2
    near = chips // 2
    group = cols // HEAD_DIM
    lines = group * rows
    me = lax.axis_index("seq")
    chip = me // 2
    core = me % 2
    partner = chip * 2 + 1 - core
    half = chip // near
    spot = chip % near
    mirror = (chip + near) % chips
    lane = me % chips

    def remote(src, dst, send, recv, device):
        return pltpu.make_async_remote_copy(
            src_ref=src,
            dst_ref=dst,
            send_sem=send,
            recv_sem=recv,
            device_id={"seq": device},
            device_id_type=pl.DeviceIdType.MESH,
        )

    def chip_at(way):
        return sum(
            ((chip // bit + way // bit) % 2) * bit for bit in (1, 2, 4)
        )

    far_first = list(range(chips - 1, 0, -1))

    def whole(ref, sem):
        return pltpu.make_async_copy(ref, ref, sem)

    barrier = pltpu.get_barrier_semaphore()
    for off in range(1, devices):
        pl.semaphore_signal(
            barrier,
            inc=1,
            device_id={"seq": (me + off) % devices},
            device_id_type=pl.DeviceIdType.MESH,
        )

    load_x = pltpu.make_async_copy(x_hbm, x_all.at[me], in_sem.at[0])
    load_mask = pltpu.make_async_copy(mask_hbm, mask_ref, in_sem.at[1])
    load_gain_one = pltpu.make_async_copy(gain_one_hbm, gain_one, in_sem.at[2])
    load_gain_two = pltpu.make_async_copy(gain_two_hbm, gain_two, in_sem.at[3])
    load_x.start()
    load_mask.start()
    stages = []
    for g in range(KV_HEADS):
        for side in range(2):
            stages.append(
                pltpu.make_async_copy(
                    kv_hbm.at[side, :, pl.ds(g * HEAD_DIM, HEAD_DIM)],
                    kv_stage.at[g // near, g % near, pl.ds(side * BLOCK, BLOCK)],
                    stage_sem,
                )
            )
            stages[-1].start()
    load_gain_one.start()
    load_gain_two.start()

    def fetch(k, src, dst):
        return pltpu.make_async_copy(src, dst, w_sem.at[k])

    fetch_q = fetch(0, q_hbm, q_w)
    fetch_o = fetch(1, o_hbm, o_w)
    fetch_gate = fetch(2, gate_hbm, gate_w)
    fetch_up = fetch(3, up_hbm, up_w)
    fetch_down = fetch(4, down_hbm, down_w)
    fetch_q.start()
    fetch_o.start()

    load_x.wait()
    with jax.named_scope("t_barrier"):
        pl.semaphore_wait(barrier, devices - 1)

    def gather_start(dst, send, near_recv, far_recv):
        for way in far_first:
            remote(
                dst.at[me], dst.at[me], send, far_recv.at[way], chip_at(way) * 2 + core
            ).start()
        remote(dst.at[me], dst.at[me], send, near_recv, partner).start()

    def gather_pass(dst, send, near_recv, far_recv):
        for way in reversed(far_first):
            other = chip_at(way) * 2 + core
            remote(dst.at[other], dst.at[other], send, far_recv.at[way], partner).wait_recv()
            remote(dst.at[other], dst.at[other], send, near_recv, partner).start()

    def gather_finish(dst, send, near_recv, far_recv):
        whole(dst.at[pl.ds(0, chips)], near_recv).wait()

    def gather_drain(dst, send, near_recv, far_recv):
        whole(dst.at[pl.ds(0, devices - 1)], send).wait()

    x_sems = (x_all, x_send, x_near, x_far)
    s_sems = (s_all, s_send, s_near, s_far)
    gather_start(*x_sems)

    load_mask.wait()
    across = lax.broadcasted_iota(jnp.int32, (rows, rows), 1)
    down = lax.broadcasted_iota(jnp.int32, (rows, rows), 0)
    for g in range(KV_HEADS):
        flat = jnp.broadcast_to(mask_ref[g].astype(jnp.float32), (rows, rows))
        column = jnp.sum(jnp.where(across == down, flat, 0.0), axis=1, keepdims=True)
        kv_stage[g // near, g % near, pl.ds(MASK_AT, rows), :] = jnp.broadcast_to(
            column, (rows, HEAD_DIM)
        ).astype(jnp.bfloat16)
    with jax.named_scope("t_stage"):
        whole(kv_stage.at[:, :, pl.ds(0, MASK_AT)], stage_sem).wait()
    own_kv = pltpu.make_async_copy(kv_stage.at[core, spot], kv_all.at[lane], kv_own_sem)
    own_kv.start()

    for k in range(chips - 1, 0, -1):
        there = chip_at(k // 2)
        side = (core + k) % 2
        remote(
            kv_stage.at[side, there % near],
            kv_all.at[lane],
            kv_send,
            kv_recv,
            there * 2 + side,
        ).start()
    fetch_gate.start()
    fetch_up.start()
    fetch_down.start()

    def norm(values, gain):
        squares = jnp.zeros((rows, cols), jnp.float32)
        for i in range(devices):
            wide = values[i].astype(jnp.float32)
            squares = squares + wide * wide
        mean = jnp.sum(squares, axis=-1, keepdims=True) * (1.0 / (devices * cols))
        inverse = lax.rsqrt(mean + eps)
        for i in range(devices):
            part_gain = gain[i * cols : (i + 1) * cols].astype(jnp.float32).reshape(1, cols)
            normed[i] = (values[i].astype(jnp.float32) * inverse * part_gain).astype(jnp.bfloat16)

    with jax.named_scope("t_xgather"):
        gather_pass(*x_sems)
        load_gain_one.wait()
        load_gain_two.wait()
        gather_finish(*x_sems)
    norm(x_all, gain_one)
    with jax.named_scope("t_fetchq"):
        fetch_q.wait()
    step = 4

    def q_step(t, total):
        for u in range(step):
            i = t * step + u
            total = total + jnp.dot(
                normed[i],
                q_w[pl.ds(pl.multiple_of(i * cols, cols), cols), :],
                preferred_element_type=jnp.float32,
            )
        return total

    with jax.named_scope("t_qmm"):
        queries = lax.fori_loop(
            0, devices // step, q_step, jnp.zeros((rows, cols), jnp.float32)
        ).astype(jnp.bfloat16)
        q_own[...] = jnp.concatenate(
            [queries[:, h * HEAD_DIM : (h + 1) * HEAD_DIM] for h in range(group)], axis=0
        )

    keeps = core == half
    to_mirror = remote(
        q_own, q_got.at[core], q_send.at[0], q_recv.at[core], mirror * 2 + half
    )
    to_partner = remote(q_own, q_got.at[core], q_send.at[1], q_recv.at[core], partner)
    to_mirror.start()

    @pl.when(jnp.logical_not(keeps))
    def _():
        to_partner.start()

    @pl.when(keeps)
    def _():
        q_got[core] = q_own[...]

    with jax.named_scope("t_kvwait"):
        own_kv.wait()
        whole(kv_all.at[pl.ds(0, chips - 1)], kv_recv).wait()

    def q_arrived(which):
        remote(q_own, q_got.at[which], q_send.at[0], q_recv.at[which], partner).wait_recv()

    with jax.named_scope("t_qwait"):
        q_arrived(1 - core)

        @pl.when(jnp.logical_not(keeps))
        def _():
            q_arrived(core)

    tops = []
    with jax.named_scope("t_attn"):
        query = jnp.concatenate([q_got[0], q_got[1]], axis=0)

        def live_at(c):
            mask = kv_all[c, pl.ds(MASK_AT, rows), :].astype(jnp.float32)
            return jnp.concatenate([mask] * (2 * group), axis=0) > 0.5

        for c in range(chips):
            score = (
                lax.dot_general(
                    query,
                    kv_all[c, pl.ds(0, BLOCK), :],
                    (((1,), (1,)), ((), ())),
                    preferred_element_type=jnp.float32,
                )
                * SCALE
            )
            masked = jnp.where(live_at(c), score, floor_score)
            scores[c] = masked
            tops.append(jnp.max(masked, axis=-1, keepdims=True))
        top = functools.reduce(jnp.maximum, tops)
        total = jnp.zeros((2 * lines, 1), jnp.float32)
        accum = jnp.zeros((2 * lines, HEAD_DIM), jnp.float32)
        for c in range(chips):
            weight = jnp.where(live_at(c), jnp.exp(scores[c] - tops[c]), 0.0)
            factor = jnp.exp(tops[c] - top)
            total = total + factor * jnp.sum(weight, axis=-1, keepdims=True)
            accum = accum + factor * jnp.dot(
                weight.astype(jnp.bfloat16),
                kv_all[c, pl.ds(BLOCK, BLOCK), :],
                preferred_element_type=jnp.float32,
            )
        row = lax.broadcasted_iota(jnp.int32, (lines, HEAD_DIM), 0)
        column = lax.broadcasted_iota(jnp.int32, (lines, HEAD_DIM), 1)
        for s in range(2):
            at = slice(s * lines, (s + 1) * lines)
            spread = jnp.where(
                column == row, top[at], jnp.where(column == row + lines, total[at], 0.0)
            )
            piece[s, pl.ds(0, lines), :] = accum[at]
            piece[s, pl.ds(lines, 8), :] = jnp.broadcast_to(
                jnp.sum(spread, axis=0, keepdims=True), (8, HEAD_DIM)
            )

    def piece_copy(which, slot, device):
        return remote(
            piece.at[which], piece_got.at[slot], piece_send.at[which], piece_recv.at[slot], device
        )

    @pl.when(keeps)
    def _():
        piece_copy(1 - core, 0, partner).start()
        piece_got[0] = piece[core]

    @pl.when(jnp.logical_not(keeps))
    def _():
        piece_copy(0, 1, mirror * 2).start()
        piece_copy(1, 1, mirror * 2 + 1).start()

    with jax.named_scope("t_piece"):

        @pl.when(jnp.logical_not(keeps))
        def _():
            piece_copy(0, 0, partner).wait_recv()

        piece_copy(0, 1, partner).wait_recv()

    with jax.named_scope("t_join"):

        def parts_of(slot):
            stats = jnp.broadcast_to(piece_got[slot, pl.ds(lines, 1), :], (lines, HEAD_DIM))
            high = jnp.sum(jnp.where(column == row, stats, 0.0), axis=1, keepdims=True)
            mass = jnp.sum(jnp.where(column == row + lines, stats, 0.0), axis=1, keepdims=True)
            return high, mass, piece_got[slot, pl.ds(0, lines), :]

        top_a, total_a, accum_a = parts_of(0)
        top_b, total_b, accum_b = parts_of(1)
        high = jnp.maximum(top_a, top_b)
        factor_a = jnp.exp(top_a - high)
        factor_b = jnp.exp(top_b - high)
        ratio = (accum_a * factor_a + accum_b * factor_b) / (
            total_a * factor_a + total_b * factor_b
        )
        attended = jnp.concatenate(
            [ratio[h * rows : (h + 1) * rows] for h in range(group)], axis=1
        ).astype(jnp.bfloat16)

    def scatter(values, weight, duo, duo_got, duo_send, duo_recv, part, got, send, recv):
        def product(to):
            return jnp.dot(
                values,
                weight[:, pl.ds(pl.multiple_of(to * cols, cols), cols)],
                preferred_element_type=jnp.float32,
            )

        def give(s):
            return remote(duo.at[s], duo_got.at[s], duo_send, duo_recv.at[s], partner)

        def post(s):
            return remote(
                part.at[s],
                got.at[chip],
                send,
                recv,
                chip_at(chips - 1 - s) * 2 + core,
            )

        def turn_one(t, _):
            @pl.when(t > 0)
            def _():
                give(2 * t - 2).start()
                give(2 * t - 1).start()

            first = product(chip_at(chips - 1 - 2 * t) * 2 + 1 - core)
            second = product(chip_at(chips - 2 - 2 * t) * 2 + 1 - core)
            duo[2 * t] = first
            duo[2 * t + 1] = second
            return 0

        def turn_two(t, _):
            @pl.when(t > 0)
            def _():
                post(2 * t - 2).start()
                post(2 * t - 1).start()

            first = product(chip_at(chips - 1 - 2 * t) * 2 + core)
            second = product(chip_at(chips - 2 - 2 * t) * 2 + core)
            give(2 * t).wait_recv()
            give(2 * t + 1).wait_recv()
            first = first + duo_got[2 * t]
            second = second + duo_got[2 * t + 1]
            part[2 * t] = first.astype(part.dtype)
            part[2 * t + 1] = second.astype(part.dtype)
            own_ref[...] = second
            return 0

        with jax.named_scope("t_prod1"):
            lax.fori_loop(0, chips // 2, turn_one, 0)
            give(chips - 2).start()
            give(chips - 1).start()
        with jax.named_scope("t_prod2"):
            lax.fori_loop(0, chips // 2, turn_two, 0)
            post(chips - 2).start()

        whole(part.at[pl.ds(0, chips - 1)], recv).wait()
        total = own_ref[...]
        for way in far_first:
            total = total + got[chip_at(way)].astype(jnp.float32)
        return total

    def scatter_drain(duo, duo_got, duo_send, duo_recv, part, got, send, recv):
        whole(duo, duo_send).wait()
        whole(part.at[pl.ds(0, chips - 1)], send).wait()

    one = (duo_one, duo_got_one, duo_send_one, duo_recv_one, part_one, got_one, send_one, recv_one)
    two = (duo_two, duo_got_two, duo_send_two, duo_recv_two, part_two, got_two, send_two, recv_two)
    with jax.named_scope("t_fetcho"):
        fetch_o.wait()
    with jax.named_scope("t_scat1"):
        attn_out = scatter(attended, o_w, *one)
    stream = (x_all[me].astype(jnp.float32) + attn_out).astype(jnp.bfloat16)
    s_all[me] = stream
    gather_start(*s_sems)
    with jax.named_scope("t_sgather"):
        gather_pass(*s_sems)
        gather_finish(*s_sems)
    norm(s_all, gain_two)
    with jax.named_scope("t_fetchgu"):
        fetch_gate.wait()
        fetch_up.wait()
    wide = gate_w.shape[1]

    def ff_step(t, sums):
        gate, upward = sums
        for u in range(2):
            i = t * 2 + u
            at = pl.ds(pl.multiple_of(i * cols, cols), cols)
            gate = gate + jnp.dot(normed[i], gate_w[at, :], preferred_element_type=jnp.float32)
            upward = upward + jnp.dot(normed[i], up_w[at, :], preferred_element_type=jnp.float32)
        return gate, upward

    zeros = jnp.zeros((rows, wide), jnp.float32)
    with jax.named_scope("t_ffmm"):
        gate, upward = lax.fori_loop(0, devices // 2, ff_step, (zeros, zeros))
    hidden = (gate / (1.0 + jnp.exp(-gate)) * upward).astype(jnp.bfloat16)
    with jax.named_scope("t_fetchd"):
        fetch_down.wait()
    with jax.named_scope("t_scat2"):
        down_out = scatter(hidden, down_w, *two)
    y_ref[...] = (s_all[me].astype(jnp.float32) + down_out).astype(jnp.bfloat16)

    with jax.named_scope("t_drain"):
        gather_drain(*x_sems)
        gather_drain(*s_sems)
        whole(kv_all.at[pl.ds(0, chips - 1)], kv_send).wait()
        to_mirror.wait_send()

        @pl.when(jnp.logical_not(keeps))
        def _():
            to_partner.wait_send()
            piece_copy(0, 1, partner).wait_send()
            piece_copy(1, 1, partner).wait_send()

        @pl.when(keeps)
        def _():
            piece_copy(1 - core, 0, partner).wait_send()

        scatter_drain(*one)
        scatter_drain(*two)


def layer(
    x_rows,
    attn_gain,
    q_weight,
    o_weight,
    mlp_gain,
    gate_weight,
    up_weight,
    down_weight,
    kv_cache,
    block_mask,
):
    rows, cols = x_rows.shape
    devices = lax.axis_size("seq")
    chips = devices // 2
    lines = rows * cols // HEAD_DIM
    dma = pltpu.SemaphoreType.DMA
    left = pl.BlockSpec(memory_space=pl.ANY)
    exchange = pltpu.VMEM((devices, rows, cols), jnp.bfloat16)
    duo = pltpu.VMEM((chips, rows, cols), jnp.float32)
    part = pltpu.VMEM((chips, rows, cols), jnp.bfloat16)
    pieces = pltpu.VMEM((2, lines + 8, HEAD_DIM), jnp.float32)
    return pl.pallas_call(
        layer_kernel,
        name="layer",
        out_shape=jax.ShapeDtypeStruct((rows, cols), jnp.bfloat16),
        in_specs=[left] * 10,
        out_specs=pl.BlockSpec(memory_space=pltpu.VMEM),
        scratch_shapes=[
            pltpu.VMEM(q_weight.shape, jnp.bfloat16),
            pltpu.VMEM(o_weight.shape, jnp.bfloat16),
            pltpu.VMEM(gate_weight.shape, jnp.bfloat16),
            pltpu.VMEM(up_weight.shape, jnp.bfloat16),
            pltpu.VMEM(down_weight.shape, jnp.bfloat16),
            pltpu.VMEM(attn_gain.shape, jnp.bfloat16),
            pltpu.VMEM(mlp_gain.shape, jnp.bfloat16),
            pltpu.VMEM((KV_HEADS, 1, rows), jnp.int32),
            exchange,
            exchange,
            exchange,
            pltpu.VMEM((2, chips // 2, MASK_AT + rows, HEAD_DIM), jnp.bfloat16),
            pltpu.VMEM((chips, MASK_AT + rows, HEAD_DIM), jnp.bfloat16),
            pltpu.VMEM((chips, 2 * lines, BLOCK), jnp.float32),
            pltpu.VMEM((lines, HEAD_DIM), jnp.bfloat16),
            pltpu.VMEM((2, lines, HEAD_DIM), jnp.bfloat16),
            pieces,
            pieces,
            *([duo, duo, part, part] * 2),
            pltpu.VMEM((rows, cols), jnp.float32),
            dma((5,)),
            dma((4,)),
            dma(()),
            dma(()),
            *([dma(()), dma(()), dma((chips,))] * 2),
            dma(()),
            dma(()),
            *([dma((2,))] * 4),
            *([dma(()), dma((chips,)), dma(()), dma(())] * 2),
        ],
        compiler_params=pltpu.CompilerParams(
            collective_id=0, has_side_effects=True, vmem_limit_bytes=67043328
        ),
    )(
        x_rows,
        attn_gain,
        q_weight,
        o_weight,
        mlp_gain,
        gate_weight,
        up_weight,
        down_weight,
        kv_cache,
        jnp.transpose(block_mask, (1, 2, 0)),
    )


def solution(mesh):
    fused = mesh.shape["seq"] == 2 * KV_HEADS
    return jax.shard_map(
        layer if fused else local,
        mesh=mesh,
        in_specs=(
            P("group", "seq"),
            P(),
            P(None, "seq"),
            P("seq", None),
            P(),
            P(None, "seq"),
            P(None, "seq"),
            P("seq", None),
            P(None, ("group", "seq"), None),
            P("group", None, "seq"),
        ),
        out_specs=P("group", "seq"),
        check_vma=False,
    )
```

```python
import functools

import jax
import jax.numpy as jnp
from jax import lax
from jax.experimental import pallas as pl
from jax.experimental.pallas import tpu as pltpu
from jax.sharding import PartitionSpec as P

HEADS = 64
KV_HEADS = 8
HEAD_DIM = 128
BLOCK = 128


eps = 1e-05
floor_score = -1e30


def combined_all(x, axis, combine):
    everything = jax.tree.map(lambda part: lax.all_gather(part, axis), x)
    initial = jax.tree.map(lambda part: part[0], everything)

    def turn(k, so_far):
        return combine(so_far, jax.tree.map(lambda part: part[k], everything))

    return lax.fori_loop(1, lax.axis_size(axis), turn, initial)


def rms_norm(values, gain):
    wide = values.astype(jnp.float32)
    inverse = lax.rsqrt(jnp.mean(wide * wide, axis=-1, keepdims=True) + eps)
    return (wide * inverse * gain.astype(jnp.float32)).astype(jnp.bfloat16)


def combine_states(first, second):
    top_a, total_a, accum_a = first
    top_b, total_b, accum_b = second
    top = jnp.maximum(top_a, top_b)
    factor_a = jnp.exp(top_a - top)
    factor_b = jnp.exp(top_b - top)
    return (
        top,
        total_a * factor_a + total_b * factor_b,
        accum_a * factor_a[..., None] + accum_b * factor_b[..., None],
    )


def local(
    x_rows,
    attn_gain,
    q_weight,
    o_weight,
    mlp_gain,
    gate_weight,
    up_weight,
    down_weight,
    kv_cache,
    block_mask,
):
    rows = x_rows.shape[0]
    group = HEADS // KV_HEADS
    key_len = kv_cache.shape[1]
    spans = key_len // BLOCK
    scale = 1.0 / HEAD_DIM**0.5
    whole = lax.all_gather(x_rows, "seq", axis=1, tiled=True)
    normed = rms_norm(whole, attn_gain)
    query_part = jnp.dot(normed, q_weight, preferred_element_type=jnp.float32).astype(jnp.bfloat16)
    queries = lax.all_gather(query_part, "seq", axis=1, tiled=True)
    doc_keys = kv_cache[0]
    doc_values = kv_cache[1]

    def one_group(index):
        query_group = lax.dynamic_slice_in_dim(
            queries, index * (group * HEAD_DIM), group * HEAD_DIM, 1
        ).reshape(rows, group, HEAD_DIM)
        key_group = lax.dynamic_slice_in_dim(doc_keys, index * HEAD_DIM, HEAD_DIM, 1)
        value_group = lax.dynamic_slice_in_dim(doc_values, index * HEAD_DIM, HEAD_DIM, 1)
        mask_group = lax.dynamic_slice_in_dim(block_mask, index, 1, 1)[:, 0, :]
        scores = (
            jnp.einsum("rhd,kd->rhk", query_group, key_group, preferred_element_type=jnp.float32)
            * scale
        )
        scores = scores.reshape(rows, group, spans, BLOCK)
        live = (mask_group == 1)[:, None, :, None]
        masked = jnp.where(live, scores, floor_score)
        local_top = jnp.max(masked, axis=(2, 3))
        weights = jnp.where(live, jnp.exp(masked - local_top[..., None, None]), 0.0)
        local_total = jnp.sum(weights, axis=(2, 3))
        rounded = weights.astype(jnp.bfloat16).reshape(rows, group, key_len)
        local_accum = jnp.einsum(
            "rhk,kd->rhd", rounded, value_group, preferred_element_type=jnp.float32
        )
        return (local_top, local_total, local_accum)

    tops, totals, accums = lax.map(one_group, jnp.arange(KV_HEADS, dtype=jnp.int32))
    local_top = jnp.moveaxis(tops, 0, 1)
    local_total = jnp.moveaxis(totals, 0, 1)
    local_accum = jnp.moveaxis(accums, 0, 1)
    columns = q_weight.shape[1]
    col_start = lax.axis_index("seq") * columns
    top, total, accum = combined_all((local_top, local_total, local_accum), "seq", combine_states)
    attended = accum / total[..., None]
    attended = attended.reshape(rows, HEADS * HEAD_DIM).astype(jnp.bfloat16)
    attn_cols = lax.dynamic_slice_in_dim(attended, col_start, columns, 1)
    weight_cols = o_weight
    attn_out = lax.psum_scatter(
        lax.dot_general(
            weight_cols, attn_cols, (((0,), (1,)), ((), ())), preferred_element_type=jnp.float32
        ),
        "seq",
        scatter_dimension=0,
        tiled=True,
    )
    stream = (x_rows.astype(jnp.float32) + attn_out.T).astype(jnp.bfloat16)
    stream_whole = lax.all_gather(stream, "seq", axis=1, tiled=True)
    normed_two = rms_norm(stream_whole, mlp_gain)
    gate = jnp.dot(normed_two, gate_weight, preferred_element_type=jnp.float32)
    upward = jnp.dot(normed_two, up_weight, preferred_element_type=jnp.float32)
    hidden = (jax.nn.silu(gate) * upward).astype(jnp.bfloat16)
    weight_cols = down_weight
    down_out = lax.psum_scatter(
        lax.dot_general(
            weight_cols, hidden, (((0,), (1,)), ((), ())), preferred_element_type=jnp.float32
        ),
        "seq",
        scatter_dimension=0,
        tiled=True,
    )
    return (stream.astype(jnp.float32) + down_out.T).astype(jnp.bfloat16)


SCALE = 1.0 / HEAD_DIM**0.5
MASK_AT = 2 * BLOCK


def layer_kernel(
    x_hbm,
    gain_one_hbm,
    q_hbm,
    o_hbm,
    gain_two_hbm,
    gate_hbm,
    up_hbm,
    down_hbm,
    kv_hbm,
    mask_hbm,
    y_ref,
    q_w,
    o_w,
    gate_w,
    up_w,
    down_w,
    gain_one,
    gain_two,
    mask_ref,
    x_all,
    s_all,
    normed,
    kv_stage,
    kv_all,
    scores,
    q_own,
    q_got,
    piece,
    piece_got,
    duo_one,
    duo_got_one,
    part_one,
    got_one,
    duo_two,
    duo_got_two,
    part_two,
    got_two,
    own_ref,
    raw,
    w_sem,
    in_sem,
    stage_sem,
    kv_own_sem,
    x_send,
    x_near,
    x_far,
    s_send,
    s_near,
    s_far,
    kv_send,
    kv_recv,
    q_send,
    q_recv,
    piece_send,
    piece_recv,
    duo_send_one,
    duo_recv_one,
    send_one,
    recv_one,
    duo_send_two,
    duo_recv_two,
    send_two,
    recv_two,
):
    devices, rows, cols = x_all.shape
    chips = devices // 2
    near = chips // 2
    group = cols // HEAD_DIM
    lines = group * rows
    me = lax.axis_index("seq")
    chip = me // 2
    core = me % 2
    partner = chip * 2 + 1 - core
    half = chip // near
    spot = chip % near
    mirror = (chip + near) % chips
    lane = me % chips

    def remote(src, dst, send, recv, device):
        return pltpu.make_async_remote_copy(
            src_ref=src,
            dst_ref=dst,
            send_sem=send,
            recv_sem=recv,
            device_id={"seq": device},
            device_id_type=pl.DeviceIdType.MESH,
        )

    def chip_at(way):
        return sum(
            ((chip // bit + way // bit) % 2) * bit for bit in (1, 2, 4)
        )

    far_first = list(range(chips - 1, 0, -1))

    def whole(ref, sem):
        return pltpu.make_async_copy(ref, ref, sem)

    barrier = pltpu.get_barrier_semaphore()
    for off in range(1, devices):
        pl.semaphore_signal(
            barrier,
            inc=1,
            device_id={"seq": (me + off) % devices},
            device_id_type=pl.DeviceIdType.MESH,
        )

    load_x = pltpu.make_async_copy(x_hbm, x_all.at[me], in_sem.at[0])
    load_mask = pltpu.make_async_copy(mask_hbm, mask_ref, in_sem.at[1])
    load_gain_one = pltpu.make_async_copy(gain_one_hbm, gain_one, in_sem.at[2])
    load_gain_two = pltpu.make_async_copy(gain_two_hbm, gain_two, in_sem.at[3])
    load_x.start()
    load_mask.start()
    stages = []
    for g in range(KV_HEADS):
        for side in range(2):
            stages.append(
                pltpu.make_async_copy(
                    kv_hbm.at[side, :, pl.ds(g * HEAD_DIM, HEAD_DIM)],
                    kv_stage.at[g // near, g % near, pl.ds(side * BLOCK, BLOCK)],
                    stage_sem,
                )
            )
            stages[-1].start()
    load_gain_one.start()
    load_gain_two.start()

    def fetch(k, src, dst):
        return pltpu.make_async_copy(src, dst, w_sem.at[k])

    fetch_q = fetch(0, q_hbm, q_w)
    fetch_o = fetch(1, o_hbm, o_w)
    fetch_gate = fetch(2, gate_hbm, gate_w)
    fetch_up = fetch(3, up_hbm, up_w)
    fetch_down = fetch(4, down_hbm, down_w)
    fetch_q.start()
    fetch_o.start()

    load_x.wait()
    with jax.named_scope("t_barrier"):
        pl.semaphore_wait(barrier, devices - 1)

    def gather_start(dst, send, near_recv, far_recv):
        for way in far_first:
            remote(
                dst.at[me], dst.at[me], send, far_recv.at[way], chip_at(way) * 2 + core
            ).start()
        remote(dst.at[me], dst.at[me], send, near_recv, partner).start()

    def gather_pass(dst, send, near_recv, far_recv):
        for way in reversed(far_first):
            other = chip_at(way) * 2 + core
            remote(dst.at[other], dst.at[other], send, far_recv.at[way], partner).wait_recv()
            remote(dst.at[other], dst.at[other], send, near_recv, partner).start()

    def gather_finish(dst, send, near_recv, far_recv):
        whole(dst.at[pl.ds(0, chips)], near_recv).wait()

    def gather_drain(dst, send, near_recv, far_recv):
        whole(dst.at[pl.ds(0, devices - 1)], send).wait()

    x_sems = (x_all, x_send, x_near, x_far)
    s_sems = (s_all, s_send, s_near, s_far)
    gather_start(*x_sems)

    load_mask.wait()
    across = lax.broadcasted_iota(jnp.int32, (rows, rows), 1)
    down = lax.broadcasted_iota(jnp.int32, (rows, rows), 0)
    for g in range(KV_HEADS):
        flat = jnp.broadcast_to(mask_ref[g].astype(jnp.float32), (rows, rows))
        column = jnp.sum(jnp.where(across == down, flat, 0.0), axis=1, keepdims=True)
        kv_stage[g // near, g % near, pl.ds(MASK_AT, rows), :] = jnp.broadcast_to(
            column, (rows, HEAD_DIM)
        ).astype(jnp.bfloat16)
    with jax.named_scope("t_stage"):
        whole(kv_stage.at[:, :, pl.ds(0, MASK_AT)], stage_sem).wait()
    own_kv = pltpu.make_async_copy(kv_stage.at[core, spot], kv_all.at[lane], kv_own_sem)
    own_kv.start()

    for k in range(chips - 1, 0, -1):
        there = chip_at(k // 2)
        side = (core + k) % 2
        remote(
            kv_stage.at[side, there % near],
            kv_all.at[lane],
            kv_send,
            kv_recv,
            there * 2 + side,
        ).start()
    fetch_gate.start()
    fetch_up.start()
    fetch_down.start()

    def norm(values, gain):
        squares = jnp.zeros((rows, cols), jnp.float32)
        for i in range(devices):
            wide = values[i].astype(jnp.float32)
            squares = squares + wide * wide
        mean = jnp.sum(squares, axis=-1, keepdims=True) * (1.0 / (devices * cols))
        inverse = lax.rsqrt(mean + eps)
        for i in range(devices):
            part_gain = gain[i * cols : (i + 1) * cols].astype(jnp.float32).reshape(1, cols)
            normed[:, i * cols : (i + 1) * cols] = (
                values[i].astype(jnp.float32) * inverse * part_gain
            ).astype(jnp.bfloat16)

    with jax.named_scope("t_xgather"):
        gather_pass(*x_sems)
        load_gain_one.wait()
        load_gain_two.wait()
        gather_finish(*x_sems)
    norm(x_all, gain_one)
    with jax.named_scope("t_fetchq"):
        fetch_q.wait()

    with jax.named_scope("t_qmm"):
        queries = jnp.dot(normed[...], q_w[...], preferred_element_type=jnp.float32).astype(
            jnp.bfloat16
        )
        q_own[...] = jnp.concatenate(
            [queries[:, h * HEAD_DIM : (h + 1) * HEAD_DIM] for h in range(group)], axis=0
        )

    keeps = core == half
    to_mirror = remote(
        q_own, q_got.at[core], q_send.at[0], q_recv.at[core], mirror * 2 + half
    )
    to_partner = remote(q_own, q_got.at[core], q_send.at[1], q_recv.at[core], partner)
    to_mirror.start()

    @pl.when(jnp.logical_not(keeps))
    def _():
        to_partner.start()

    @pl.when(keeps)
    def _():
        q_got[core] = q_own[...]

    with jax.named_scope("t_kvwait"):
        own_kv.wait()
        whole(kv_all.at[pl.ds(0, chips - 1)], kv_recv).wait()

    def q_arrived(which):
        remote(q_own, q_got.at[which], q_send.at[0], q_recv.at[which], partner).wait_recv()

    with jax.named_scope("t_qwait"):
        q_arrived(1 - core)

        @pl.when(jnp.logical_not(keeps))
        def _():
            q_arrived(core)

    tops = []
    with jax.named_scope("t_attn"):
        query = jnp.concatenate([q_got[0], q_got[1]], axis=0)

        def live_at(c):
            mask = kv_all[c, pl.ds(MASK_AT, rows), :].astype(jnp.float32)
            return jnp.concatenate([mask] * (2 * group), axis=0) > 0.5

        for c in range(chips):
            score = (
                lax.dot_general(
                    query,
                    kv_all[c, pl.ds(0, BLOCK), :],
                    (((1,), (1,)), ((), ())),
                    preferred_element_type=jnp.float32,
                )
                * SCALE
            )
            masked = jnp.where(live_at(c), score, floor_score)
            scores[c] = masked
            tops.append(jnp.max(masked, axis=-1, keepdims=True))
        top = functools.reduce(jnp.maximum, tops)
        total = jnp.zeros((2 * lines, 1), jnp.float32)
        accum = jnp.zeros((2 * lines, HEAD_DIM), jnp.float32)
        for c in range(chips):
            weight = jnp.where(live_at(c), jnp.exp(scores[c] - tops[c]), 0.0)
            factor = jnp.exp(tops[c] - top)
            total = total + factor * jnp.sum(weight, axis=-1, keepdims=True)
            accum = accum + factor * jnp.dot(
                weight.astype(jnp.bfloat16),
                kv_all[c, pl.ds(BLOCK, BLOCK), :],
                preferred_element_type=jnp.float32,
            )
        row = lax.broadcasted_iota(jnp.int32, (lines, HEAD_DIM), 0)
        column = lax.broadcasted_iota(jnp.int32, (lines, HEAD_DIM), 1)
        for s in range(2):
            at = slice(s * lines, (s + 1) * lines)
            spread = jnp.where(
                column == row, top[at], jnp.where(column == row + lines, total[at], 0.0)
            )
            piece[s, pl.ds(0, lines), :] = accum[at]
            piece[s, pl.ds(lines, 8), :] = jnp.broadcast_to(
                jnp.sum(spread, axis=0, keepdims=True), (8, HEAD_DIM)
            )

    def piece_copy(which, slot, device):
        return remote(
            piece.at[which], piece_got.at[slot], piece_send.at[which], piece_recv.at[slot], device
        )

    @pl.when(keeps)
    def _():
        piece_copy(1 - core, 0, partner).start()
        piece_got[0] = piece[core]

    @pl.when(jnp.logical_not(keeps))
    def _():
        piece_copy(0, 1, mirror * 2).start()
        piece_copy(1, 1, mirror * 2 + 1).start()

    with jax.named_scope("t_piece"):

        @pl.when(jnp.logical_not(keeps))
        def _():
            piece_copy(0, 0, partner).wait_recv()

        piece_copy(0, 1, partner).wait_recv()

    with jax.named_scope("t_join"):

        def parts_of(slot):
            stats = jnp.broadcast_to(piece_got[slot, pl.ds(lines, 1), :], (lines, HEAD_DIM))
            high = jnp.sum(jnp.where(column == row, stats, 0.0), axis=1, keepdims=True)
            mass = jnp.sum(jnp.where(column == row + lines, stats, 0.0), axis=1, keepdims=True)
            return high, mass, piece_got[slot, pl.ds(0, lines), :]

        top_a, total_a, accum_a = parts_of(0)
        top_b, total_b, accum_b = parts_of(1)
        high = jnp.maximum(top_a, top_b)
        factor_a = jnp.exp(top_a - high)
        factor_b = jnp.exp(top_b - high)
        ratio = (accum_a * factor_a + accum_b * factor_b) / (
            total_a * factor_a + total_b * factor_b
        )
        attended = jnp.concatenate(
            [ratio[h * rows : (h + 1) * rows] for h in range(group)], axis=1
        ).astype(jnp.bfloat16)

    def scatter(lag, values, weight, duo, duo_got, duo_send, duo_recv, part, got, send, recv):
        def product(to):
            return jnp.dot(
                values,
                weight[:, pl.ds(pl.multiple_of(to * cols, cols), cols)],
                preferred_element_type=jnp.float32,
            )

        def give(s):
            return remote(duo.at[s], duo_got.at[s], duo_send, duo_recv.at[s], partner)

        def post(s):
            return remote(
                part.at[s],
                got.at[chip],
                send,
                recv,
                chip_at(chips - 1 - s) * 2 + core,
            )

        def finish(s):
            give(s).wait_recv()
            both = raw[s] + duo_got[s]
            if s == chips - 1:
                own_ref[...] = both
            else:
                part[s] = both.astype(part.dtype)
            if s > 0:
                post(s - 1).start()

        before = None
        with jax.named_scope("t_prod"):
            for turn in range(2 * chips):
                s = turn % chips
                to = chip_at(chips - 1 - s) * 2
                now = product(to + 1 - core if turn < chips else to + core)
                if turn > 0:
                    store = duo if turn <= chips else raw
                    store[(turn - 1) % chips] = before
                if 2 <= turn < chips + 2:
                    give(turn - 2).start()
                if turn - chips >= lag:
                    finish(turn - chips - lag)
                before = now
            raw[chips - 1] = before
        with jax.named_scope("t_fin"):
            for s in range(chips - lag, chips):
                finish(s)

        whole(part.at[pl.ds(0, chips - 1)], recv).wait()
        total = own_ref[...]
        for way in far_first:
            total = total + got[chip_at(way)].astype(jnp.float32)
        return total

    def scatter_drain(duo, duo_got, duo_send, duo_recv, part, got, send, recv):
        whole(duo, duo_send).wait()
        whole(part.at[pl.ds(0, chips - 1)], send).wait()

    one = (duo_one, duo_got_one, duo_send_one, duo_recv_one, part_one, got_one, send_one, recv_one)
    two = (duo_two, duo_got_two, duo_send_two, duo_recv_two, part_two, got_two, send_two, recv_two)
    with jax.named_scope("t_fetcho"):
        fetch_o.wait()
    with jax.named_scope("t_scat1"):
        attn_out = scatter(chips, attended, o_w, *one)
    stream = (x_all[me].astype(jnp.float32) + attn_out).astype(jnp.bfloat16)
    s_all[me] = stream
    gather_start(*s_sems)
    with jax.named_scope("t_sgather"):
        gather_pass(*s_sems)
        gather_finish(*s_sems)
    norm(s_all, gain_two)
    with jax.named_scope("t_fetchgu"):
        fetch_gate.wait()
        fetch_up.wait()

    with jax.named_scope("t_ffmm"):
        gate = jnp.dot(normed[...], gate_w[...], preferred_element_type=jnp.float32)
        upward = jnp.dot(normed[...], up_w[...], preferred_element_type=jnp.float32)
    hidden = (gate / (1.0 + jnp.exp(-gate)) * upward).astype(jnp.bfloat16)
    with jax.named_scope("t_fetchd"):
        fetch_down.wait()
    with jax.named_scope("t_scat2"):
        down_out = scatter(chips // 2, hidden, down_w, *two)
    y_ref[...] = (s_all[me].astype(jnp.float32) + down_out).astype(jnp.bfloat16)

    with jax.named_scope("t_drain"):
        gather_drain(*x_sems)
        gather_drain(*s_sems)
        whole(kv_all.at[pl.ds(0, chips - 1)], kv_send).wait()
        to_mirror.wait_send()

        @pl.when(jnp.logical_not(keeps))
        def _():
            to_partner.wait_send()
            piece_copy(0, 1, partner).wait_send()
            piece_copy(1, 1, partner).wait_send()

        @pl.when(keeps)
        def _():
            piece_copy(1 - core, 0, partner).wait_send()

        scatter_drain(*one)
        scatter_drain(*two)


def layer(
    x_rows,
    attn_gain,
    q_weight,
    o_weight,
    mlp_gain,
    gate_weight,
    up_weight,
    down_weight,
    kv_cache,
    block_mask,
):
    rows, cols = x_rows.shape
    devices = lax.axis_size("seq")
    chips = devices // 2
    lines = rows * cols // HEAD_DIM
    dma = pltpu.SemaphoreType.DMA
    left = pl.BlockSpec(memory_space=pl.ANY)
    exchange = pltpu.VMEM((devices, rows, cols), jnp.bfloat16)
    duo = pltpu.VMEM((chips, rows, cols), jnp.float32)
    part = pltpu.VMEM((chips, rows, cols), jnp.bfloat16)
    pieces = pltpu.VMEM((2, lines + 8, HEAD_DIM), jnp.float32)
    return pl.pallas_call(
        layer_kernel,
        name="layer",
        out_shape=jax.ShapeDtypeStruct((rows, cols), jnp.bfloat16),
        in_specs=[left] * 10,
        out_specs=pl.BlockSpec(memory_space=pltpu.VMEM),
        scratch_shapes=[
            pltpu.VMEM(q_weight.shape, jnp.bfloat16),
            pltpu.VMEM(o_weight.shape, jnp.bfloat16),
            pltpu.VMEM(gate_weight.shape, jnp.bfloat16),
            pltpu.VMEM(up_weight.shape, jnp.bfloat16),
            pltpu.VMEM(down_weight.shape, jnp.bfloat16),
            pltpu.VMEM(attn_gain.shape, jnp.bfloat16),
            pltpu.VMEM(mlp_gain.shape, jnp.bfloat16),
            pltpu.VMEM((KV_HEADS, 1, rows), jnp.int32),
            exchange,
            exchange,
            pltpu.VMEM((rows, devices * cols), jnp.bfloat16),
            pltpu.VMEM((2, chips // 2, MASK_AT + rows, HEAD_DIM), jnp.bfloat16),
            pltpu.VMEM((chips, MASK_AT + rows, HEAD_DIM), jnp.bfloat16),
            pltpu.VMEM((chips, 2 * lines, BLOCK), jnp.float32),
            pltpu.VMEM((lines, HEAD_DIM), jnp.bfloat16),
            pltpu.VMEM((2, lines, HEAD_DIM), jnp.bfloat16),
            pieces,
            pieces,
            *([duo, duo, part, part] * 2),
            pltpu.VMEM((rows, cols), jnp.float32),
            duo,
            dma((5,)),
            dma((4,)),
            dma(()),
            dma(()),
            *([dma(()), dma(()), dma((chips,))] * 2),
            dma(()),
            dma(()),
            *([dma((2,))] * 4),
            *([dma(()), dma((chips,)), dma(()), dma(())] * 2),
        ],
        compiler_params=pltpu.CompilerParams(
            collective_id=0, has_side_effects=True, vmem_limit_bytes=67043328
        ),
    )(
        x_rows,
        attn_gain,
        q_weight,
        o_weight,
        mlp_gain,
        gate_weight,
        up_weight,
        down_weight,
        kv_cache,
        jnp.transpose(block_mask, (1, 2, 0)),
    )


def solution(mesh):
    fused = mesh.shape["seq"] == 2 * KV_HEADS
    return jax.shard_map(
        layer if fused else local,
        mesh=mesh,
        in_specs=(
            P("group", "seq"),
            P(),
            P(None, "seq"),
            P("seq", None),
            P(),
            P(None, "seq"),
            P(None, "seq"),
            P("seq", None),
            P(None, ("group", "seq"), None),
            P("group", None, "seq"),
        ),
        out_specs=P("group", "seq"),
        check_vma=False,
    )
```
